32 devices in a mesh: gx: 8 (over y, x, core), gy: 4 (over z).
Axes of the slice: x: 2, y: 2, z: 4, core: 2. Of those that a mesh axis runs over, the one named last changes fastest.
Arguments:
- velocity: float32 [3, 1, 384, 1024], P(None, None, 'gy', 'gx'), may hold values from -6 to 6
- block_inverse: float32 [384, 96], P('gy'), may hold values from -1.6 to 1.6, as said below
- lower_map: float32 [384, 96], P('gy'), may hold values from -1 to 1
- upper_map: float32 [384, 96], P('gy'), may hold values from -1 to 1
Outputs:
- new_velocity: float32 [3, 1, 384, 2048], P(None, None, 'gy', 'gx')
The draws below stay inside these ranges and needn't reach their ends.
Inputs may be any that keep to these rules, and one draw needn't show every extreme that they name: `block_inverse`: entries of the given block inverses.
All inputs are finite; a program needn't handle non-finite values.
Results may differ from the reference program's by a relative error of at most 0.00012.
Values sent between devices are 32-bit elements; how exact they have to be, the bound alone decides.
A program may use at most 64 MiB of HBM per device.

```python
import math
import jax
import jax.numpy as jnp
import numpy as np
from jax import lax

XLOC = 128
YLOC = 96
PLANES = 1
NX = 1024
NY = 384
N_GX = 8
N_GY = 4


def coupling_draw(key, diag_low, diag_high, spread):
    keys = jax.random.split(key, 2)
    row_place = jnp.arange(NY) % YLOC
    on_diagonal = row_place[:, None] == jnp.arange(YLOC)[None, :]
    diagonal = jnp.exp(jax.random.uniform(keys[0], (NY, 1), jnp.float32, math.log(diag_low), math.log(diag_high)))
    noise = jnp.clip(jax.random.normal(keys[1], (NY, YLOC), jnp.float32), -4.0, 4.0)
    return jnp.where(on_diagonal, diagonal, noise * (spread / math.sqrt(YLOC))).astype(jnp.float32)


def draw_block_inverse(key, part):
    return coupling_draw(jax.random.fold_in(key, 11), 0.5, 1.5, 0.3)


def draw_lower_map(key, part):
    return coupling_draw(jax.random.fold_in(key, 23), 0.4, 0.97, 0.15)


def draw_upper_map(key, part):
    return coupling_draw(jax.random.fold_in(key, 37), 0.4, 0.97, 0.15)


def shard_levels(own_key, shape, shards, smallest, high):
    loudness = 1.0
    for dim, shards_of in shards:
        draws = jax.random.uniform(jax.random.fold_in(jax.random.fold_in(own_key, 6), dim), (shards_of,), jnp.float32, smallest / len(shards), high / len(shards))
        loudness = loudness * jnp.repeat(jnp.exp(draws), shape[dim] // shards_of).reshape((-1,) + (1,) * (len(shape) - 1 - dim))
    return loudness


def centred(stream_key, extent, width, reach, cuts=(), held_as=jnp.bfloat16):
    values = width * jax.random.normal(stream_key, extent, jnp.float32)
    if cuts:
        values = values * shard_levels(stream_key, extent, cuts, -0.22, 0.18)
    return jnp.clip(values, -reach, reach).astype(held_as)


def setup_inputs(seed: int = 0) -> dict:
    splits = jax.random.split(jax.random.key(seed), 5)
    return {
        "velocity": centred(splits[0], (3, PLANES, NY, NX), 1.0, 6.0, ((2, 4), (3, 8)), jnp.float32),
        "block_inverse": draw_block_inverse(jax.random.fold_in(splits[4], 71), 0),
        "lower_map": draw_lower_map(jax.random.fold_in(splits[4], 71), 0),
        "upper_map": draw_upper_map(jax.random.fold_in(splits[4], 71), 0),
    }


courant = 0.8


def reverse_bits(position, levels):
    result = position * 0
    for digit_place in range(levels):
        result = result + ((position >> digit_place) & 1) * (1 << (levels - 1 - digit_place))
    return result


def advance(matrix, state):
    return jnp.einsum("ab,spbw->spaw", matrix, state, precision=lax.Precision.HIGHEST)


def reference(velocity, block_inverse, lower_map, upper_map):
    fluxes = velocity[0:1] * velocity
    fields = jnp.concatenate([velocity, fluxes], 0)
    spectrum = jnp.fft.fft(fields, axis=-1, norm="ortho")
    levels = N_GX.bit_length() - 1
    owners = np.arange(N_GX)
    leading = reverse_bits(owners, levels)
    wavenumbers = (leading[:, None] + N_GX * np.arange(XLOC)[None, :]).reshape(-1)
    spectrum = spectrum[..., wavenumbers]
    signed = np.where(wavenumbers < NX // 2, wavenumbers, wavenumbers - NX)
    factor = jnp.asarray(courant * signed / (NX // 2), jnp.float32)
    real_part = jnp.real(spectrum).astype(jnp.float32)
    imag_part = jnp.imag(spectrum).astype(jnp.float32)
    side_real = real_part[:3] + factor * imag_part[3:]
    side_imag = imag_part[:3] - factor * real_part[3:]
    right_side = jnp.stack([side_real.reshape(3, PLANES, NY, N_GX, XLOC), side_imag.reshape(3, PLANES, NY, N_GX, XLOC)], 4)
    right_side = right_side.reshape(3, PLANES, NY, 2 * NX)
    blocks = jnp.moveaxis(right_side.reshape(3, PLANES, N_GY, YLOC, 2 * NX), 2, 0)
    inverses = block_inverse.reshape(N_GY, YLOC, YLOC)
    lowers = lower_map.reshape(N_GY, YLOC, YLOC)
    uppers = upper_map.reshape(N_GY, YLOC, YLOC)
    loads = jnp.einsum("jab,jspbw->jspaw", inverses, blocks, precision=lax.Precision.HIGHEST)

    def down_step(state_prev, inputs):
        fresh = inputs[1] + advance(inputs[0], state_prev)
        return fresh, fresh

    def up_step(state_prev, inputs):
        fresh = inputs[1] + advance(inputs[0], state_prev)
        return fresh, fresh

    start_state = jnp.zeros((3, PLANES, YLOC, 2 * NX), jnp.float32)
    unused, sweeps = lax.scan(down_step, start_state, (lowers, loads))
    unused, solved = lax.scan(up_step, start_state, (uppers, sweeps), reverse=True)
    return jnp.moveaxis(solved, 0, 2).reshape(3, PLANES, NY, 2 * NX)
```

```python
import functools
import math

import jax
import jax.numpy as jnp
from jax import lax
from jax.experimental import pallas as pl
from jax.experimental.pallas import tpu as pltpu
from jax.sharding import PartitionSpec as P

courant = 0.8
HIGHEST = lax.Precision.HIGHEST


def split(x):
    high = x.astype(jnp.bfloat16)
    return high, (x - high.astype(jnp.float32)).astype(jnp.bfloat16)


def dot3(a, b):
    dot = functools.partial(jnp.dot, preferred_element_type=jnp.float32)
    return dot(a[0], b[0]) + (dot(a[0], b[1]) + dot(a[1], b[0]))


def dot_full(a, b):
    return jnp.dot(a, b, precision=HIGHEST, preferred_element_type=jnp.float32)


def reversed_position(position, levels):
    result = position * 0
    for place in range(levels):
        result = result + ((position >> place) & 1) * (1 << (levels - 1 - place))
    return result


def kernel(
    n_gx, n_gy, chunk,
    v_ref, b_ref, l_ref, r_ref, o_ref,
    gat, coef, table, acc, g_in, g_out, stack, chain,
    d_in, d_out, u_in, u_out,
    gx_send, gx_recv, g_send, g_recv, d_send, d_recv, u_send, u_recv,
):
    items, rows, local_x = v_ref.shape
    planes = items // 3
    half = rows // 2
    levels = n_gx.bit_length() - 1
    total_x = local_x * n_gx
    me = lax.axis_index("gx")
    z = lax.axis_index("gy")
    lead = reversed_position(me, levels)
    first, last = z == 0, z == n_gy - 1

    barrier = pltpu.get_barrier_semaphore()
    for place in range(levels):
        pl.semaphore_signal(barrier, inc=1, device_id={"gx": me ^ (1 << place)}, device_id_type=pl.DeviceIdType.MESH)

    @pl.when(z > 0)
    def _():
        pl.semaphore_signal(barrier, inc=1, device_id={"gy": z - 1}, device_id_type=pl.DeviceIdType.MESH)

    @pl.when(z < n_gy - 1)
    def _():
        pl.semaphore_signal(barrier, inc=1, device_id={"gy": z + 1}, device_id_type=pl.DeviceIdType.MESH)

    peers = levels + jnp.where(z > 0, 1, 0) + jnp.where(z < n_gy - 1, 1, 0)
    pl.semaphore_wait(barrier, peers)

    outer = [1 << place for place in reversed(range(1, levels))]
    turn = len(outer) // 2
    orders = [outer + [1], outer[turn:] + outer[:turn] + [1]]
    if levels == 0:
        orders = [[], []]

    def piece(part, mask):
        span = pl.ds(part * half, half)
        return v_ref.at[:, span, :] if mask == 0 else gat.at[mask, :, span, :]

    def copy(part, mask, bit):
        return pltpu.make_async_remote_copy(
            src_ref=piece(part, mask),
            dst_ref=gat.at[mask | bit, :, pl.ds(part * half, half), :],
            send_sem=gx_send.at[part, mask | bit],
            recv_sem=gx_recv.at[part, mask | bit],
            device_id={"gx": me ^ bit},
            device_id_type=pl.DeviceIdType.MESH,
        )

    def last_bit(part, mask):
        return [bit for bit in orders[part] if mask & bit][-1]

    def forward(part, mask):
        order = orders[part]
        begin = order.index(last_bit(part, mask)) + 1 if mask else 0
        for bit in order[begin:]:
            copy(part, mask, bit).start()

    def arrive(part, mask):
        bit = last_bit(part, mask)
        copy(part, mask ^ bit, bit).wait_recv()

    for part in range(2):
        forward(part, 0)

    def g_copy():
        return pltpu.make_async_remote_copy(
            src_ref=g_out, dst_ref=g_in, send_sem=g_send, recv_sem=g_recv,
            device_id={"gy": jnp.maximum(z - 1, 0)}, device_id_type=pl.DeviceIdType.MESH,
        )

    def keep_matrices(hb):
        for ref, top, low in ((stack, b_ref[...], hb), (chain, l_ref[...], g_out[...])):
            both = split(jnp.concatenate([top, low], 0))
            ref[0], ref[1] = both

    @pl.when(last)
    def _():
        g_out[...] = l_ref[...]
        if n_gy > 1:
            g_copy().start()
        keep_matrices(b_ref[...])

    def g_step():
        g_copy().wait_recv()
        inner = dot_full(r_ref[...], g_in[...])
        g_out[...] = l_ref[...] + dot_full(inner, l_ref[...])

        @pl.when(z > 0)
        def _():
            g_copy().start()

        keep_matrices(b_ref[...] + dot_full(inner, b_ref[...]))

    masks = lax.broadcasted_iota(jnp.int32, coef.shape[1:], 0)
    turns = ((masks ^ me) * lead) & (n_gx - 1)
    angles = turns.astype(jnp.float32) * (2.0 * math.pi / n_gx)
    coef[0] = jnp.cos(angles)
    coef[1] = -jnp.sin(angles)
    cells = lax.broadcasted_iota(jnp.int32, (local_x, local_x), 0)
    waves = lead + n_gx * lax.broadcasted_iota(jnp.int32, (local_x, local_x), 1)
    phases = ((cells * waves) & (total_x - 1)).astype(jnp.float32) * (2.0 * math.pi / total_x)
    scale = 1.0 / math.sqrt(total_x)
    cosine = jnp.cos(phases) * scale
    sine = jnp.sin(phases) * scale
    signed = jnp.where(waves < total_x // 2, waves, waves - total_x)
    rate = courant * signed.astype(jnp.float32) / (total_x // 2)
    quarters = (
        (cosine, -sine), (sine, cosine),
        (-rate * sine, -rate * cosine), (rate * cosine, -rate * sine),
    )
    for i, pair in enumerate(quarters):
        for j, values in enumerate(pair):
            where = (pl.ds(i * local_x, local_x), pl.ds(j * local_x, local_x))
            high, low = split(values)
            table[(0,) + where] = high
            table[(1,) + where] = low

    def absorb(group, fresh):
        leads = [v_ref[s] if m == 0 else gat[m, s] for m in group for s in range(planes)]
        for i in range(items):
            sums = [None] * 4
            for at, m in enumerate(group):
                own = v_ref[i] if m == 0 else gat[m, i]
                flux = own * leads[at * planes + i % planes]
                c, s = coef[0, m : m + 1, :], coef[1, m : m + 1, :]
                for k, term in enumerate((own * c, own * s, flux * c, flux * s)):
                    sums[k] = term if sums[k] is None else sums[k] + term
            for k in range(4):
                lanes = pl.ds(k * local_x, local_x)
                if fresh:
                    acc[i, :, lanes] = sums[k]
                else:
                    acc[i, :, lanes] = acc[i, :, lanes] + sums[k]

    if n_gy > 1:
        pl.when(z == n_gy - 2)(g_step)
    absorb([0], True)
    by_hops = {}
    for m in range(1, n_gx):
        by_hops.setdefault(((m >> 1).bit_count(), m & 1), []).append(m)
    for at, key in enumerate(sorted(by_hops)):
        group = by_hops[key]
        for m in group:
            for part in range(2):
                arrive(part, m)
                forward(part, m)
        for begin in range(0, len(group), 2):
            absorb(group[begin : begin + 2], False)
        if n_gy > 2 and key == (1, 0):
            pl.when(z == n_gy - 3)(g_step)
    if n_gy > 3:
        pl.when(z < n_gy - 3)(g_step)

    width = 2 * local_x
    per_item = width // chunk
    count = items * per_item

    def chain_copy(down, c):
        src, dst, send, recv = (d_out, d_in, d_send, d_recv) if down else (u_out, u_in, u_send, u_recv)
        to = jnp.minimum(z + 1, n_gy - 1) if down else jnp.maximum(z - 1, 0)
        return pltpu.make_async_remote_copy(
            src_ref=src.at[c], dst_ref=dst.at[c], send_sem=send.at[c], recv_sem=recv.at[c],
            device_id={"gy": to}, device_id_type=pl.DeviceIdType.MESH,
        )

    def lanes_of(c):
        return c // per_item, pl.ds((c % per_item) * chunk, chunk)

    for i in range(items):
        side = split(dot3(split(acc[i]), (table[0], table[1])))
        both = dot3((stack[0], stack[1]), side)
        o_ref[i] = both[rows:]
        for k in range(per_item):
            c = i * per_item + k
            d_out[c] = both[:rows, k * chunk : (k + 1) * chunk]
            u_out[c] = both[rows:, k * chunk : (k + 1) * chunk]

            if n_gy > 1:
                @pl.when(first)
                def _():
                    chain_copy(True, c).start()

                @pl.when(last)
                def _():
                    chain_copy(False, c).start()

    def step_down(c):
        i, lanes = lanes_of(c)

        @pl.when(z > 0)
        def _():
            chain_copy(True, c).wait_recv()
            got = dot3((chain[0], chain[1]), split(d_in[c]))

            @pl.when(z < n_gy - 1)
            def _():
                d_out[c] = d_out[c] + got[:rows]
                chain_copy(True, c).start()

            o_ref[i, :, lanes] = o_ref[i, :, lanes] + got[rows:]

    upper = split(r_ref[...])

    def step_up(c):
        i, lanes = lanes_of(c)

        @pl.when(z < n_gy - 1)
        def _():
            chain_copy(False, c).wait_recv()
            got = dot3(upper, split(u_in[c]))

            @pl.when(z > 0)
            def _():
                u_out[c] = u_out[c] + got
                chain_copy(False, c).start()

            o_ref[i, :, lanes] = o_ref[i, :, lanes] + got

    lag = min(3, count)
    if n_gy > 1:
        for early, late, here in (
            (step_down, step_up, z < n_gy // 2),
            (step_up, step_down, z >= n_gy // 2),
        ):
            @pl.when(here)
            def _():
                for s in range(count + lag):
                    if s < count:
                        early(s)
                    if s >= lag:
                        late(s - lag)

    for part in range(2):
        for m in range(1, n_gx):
            bit = last_bit(part, m)
            copy(part, m ^ bit, bit).wait_send()
    if n_gy > 1:
        @pl.when(z > 0)
        def _():
            g_copy().wait_send()
            for c in range(count):
                chain_copy(False, c).wait_send()

        @pl.when(z < n_gy - 1)
        def _():
            for c in range(count):
                chain_copy(True, c).wait_send()


def shards(velocity, block_inverse, lower_map, upper_map):
    comps, planes, rows, local_x = velocity.shape
    n_gx, n_gy = lax.axis_size("gx"), lax.axis_size("gy")
    items = comps * planes
    chunk = local_x
    count = items * 2 * local_x // chunk
    f32, bf16 = jnp.float32, jnp.bfloat16
    vmem, dma = pltpu.VMEM, pltpu.SemaphoreType.DMA
    out = pl.pallas_call(
        functools.partial(kernel, n_gx, n_gy, chunk),
        out_shape=jax.ShapeDtypeStruct((items, rows, 2 * local_x), f32),
        in_specs=[pl.BlockSpec(memory_space=pltpu.VMEM)] * 4,
        out_specs=pl.BlockSpec(memory_space=pltpu.VMEM),
        scratch_shapes=[
            vmem((n_gx, items, rows, local_x), f32),
            vmem((2, max(n_gx, 8), local_x), f32),
            vmem((2, 4 * local_x, 2 * local_x), bf16),
            vmem((items, rows, 4 * local_x), f32),
            vmem((rows, rows), f32),
            vmem((rows, rows), f32),
            vmem((2, 2 * rows, rows), bf16),
            vmem((2, 2 * rows, rows), bf16),
            vmem((count, rows, chunk), f32),
            vmem((count, rows, chunk), f32),
            vmem((count, rows, chunk), f32),
            vmem((count, rows, chunk), f32),
            dma((2, n_gx)), dma((2, n_gx)), dma, dma,
            dma((count,)), dma((count,)), dma((count,)), dma((count,)),
        ],
        compiler_params=pltpu.CompilerParams(
            collective_id=0, has_side_effects=True, vmem_limit_bytes=48 * 2**20
        ),
        name="step",
    )(velocity.reshape(items, rows, local_x), block_inverse, lower_map, upper_map)
    return out.reshape(comps, planes, rows, 2 * local_x)


def solution(mesh):
    return jax.shard_map(
        shards,
        mesh=mesh,
        in_specs=(P(None, None, "gy", "gx"), P("gy", None), P("gy", None), P("gy", None)),
        out_specs=P(None, None, "gy", "gx"),
        check_vma=False,
    )
```

```python
import functools
import math

import jax
import jax.numpy as jnp
from jax import lax
from jax.experimental import pallas as pl
from jax.experimental.pallas import tpu as pltpu
from jax.sharding import PartitionSpec as P

courant = 0.8


def split(x):
    high = x.astype(jnp.bfloat16)
    return high, (x - high.astype(jnp.float32)).astype(jnp.bfloat16)


def dot3(a, b):
    dot = functools.partial(jnp.dot, preferred_element_type=jnp.float32)
    return dot(a[0], b[0]) + (dot(a[0], b[1]) + dot(a[1], b[0]))


def reversed_position(position, levels):
    result = position * 0
    for place in range(levels):
        result = result + ((position >> place) & 1) * (1 << (levels - 1 - place))
    return result


def kernel(
    n_gx, n_gy, chunk,
    v_hbm, b_hbm, l_hbm, r_hbm, o_ref,
    v_ref, b_ref, l_ref, r_ref, gat, coef, table, acc, g_in, g_out,
    d_in, d_out, u_in, u_out, across,
    own_sem, map_sem, gx_send, gx_recv, g_send, g_recv, d_send, d_recv, u_send, u_recv,
):
    items, rows, local_x = v_ref.shape
    planes = items // 3
    half = rows // 2
    levels = n_gx.bit_length() - 1
    hops = max(levels - 1, 0)
    total_x = local_x * n_gx
    me = lax.axis_index("gx")
    z = lax.axis_index("gy")
    lead = reversed_position(me, levels)
    first, last = z == 0, z == n_gy - 1
    mesh_type = pl.DeviceIdType.MESH

    own = [pltpu.make_async_copy(v_hbm.at[i], v_ref.at[i], own_sem.at[i]) for i in range(items)]
    maps = [
        pltpu.make_async_copy(src, dst, map_sem.at[i])
        for i, (src, dst) in enumerate(((l_hbm, l_ref), (r_hbm, r_ref), (b_hbm, b_ref)))
    ]
    for local in own + maps:
        local.start()

    barrier = pltpu.get_barrier_semaphore()
    for place in range(levels):
        pl.semaphore_signal(barrier, inc=1, device_id={"gx": me ^ (1 << place)}, device_id_type=mesh_type)

    @pl.when(z > 0)
    def _():
        pl.semaphore_signal(barrier, inc=1, device_id={"gy": z - 1}, device_id_type=mesh_type)

    @pl.when(z < n_gy - 1)
    def _():
        pl.semaphore_signal(barrier, inc=1, device_id={"gy": z + 1}, device_id_type=mesh_type)

    for local in own + maps:
        local.wait()
    peers = levels + jnp.where(z > 0, 1, 0) + jnp.where(z < n_gy - 1, 1, 0)
    pl.semaphore_wait(barrier, peers)

    outer = [1 << place for place in reversed(range(1, levels))]
    turn = len(outer) // 2
    orders = [outer + [1], outer[turn:] + outer[:turn] + [1]]

    def copy(item, part, mask, bit):
        span = pl.ds(part * half, half)
        return pltpu.make_async_remote_copy(
            src_ref=gat.at[mask, item, span, :] if mask else v_ref.at[item, span, :],
            dst_ref=gat.at[mask | bit, item, span, :],
            send_sem=gx_send.at[item, part, mask | bit],
            recv_sem=gx_recv.at[item, part, mask | bit],
            device_id={"gx": me ^ bit},
            device_id_type=mesh_type,
        )

    def last_bit(part, mask):
        return [bit for bit in orders[part] if mask & bit][-1]

    def arrive(item, part, mask):
        bit = last_bit(part, mask)
        copy(item, part, mask ^ bit, bit).wait_recv()

    def forward(item, masks):
        for mask in masks:
            begins = []
            for part in range(2):
                if mask:
                    arrive(item, part, mask)
                begins.append(orders[part].index(last_bit(part, mask)) + 1 if mask else 0)
            for at in range(len(orders[0])):
                for part in range(2):
                    if at >= begins[part]:
                        copy(item, part, mask, orders[part][at]).start()

    if n_gx > 1:
        for item in range(items if hops == 0 else min(2, items)):
            forward(item, [0])

    def g_copy():
        return pltpu.make_async_remote_copy(
            src_ref=g_out, dst_ref=g_in, send_sem=g_send, recv_sem=g_recv,
            device_id={"gy": jnp.maximum(z - 1, 0)}, device_id_type=mesh_type,
        )

    if n_gy > 1:
        @pl.when(last)
        def _():
            g_out[...] = l_ref[...]
            g_copy().start()

    def g_step():
        g_copy().wait_recv()

        @pl.when(z > 0)
        def _():
            low = l_ref[...]
            inner = dot3(split(g_in[...]), split(low))
            g_out[...] = low + dot3(split(r_ref[...]), split(inner))
            g_copy().start()

    masks = lax.broadcasted_iota(jnp.int32, coef.shape[1:], 0)
    turns = ((masks ^ me) * lead) & (n_gx - 1)
    angles = turns.astype(jnp.float32) * (2.0 * math.pi / n_gx)
    coef[0] = jnp.cos(angles)
    coef[1] = -jnp.sin(angles)
    cells = lax.broadcasted_iota(jnp.int32, (local_x, local_x), 0)
    waves = lead + n_gx * lax.broadcasted_iota(jnp.int32, (local_x, local_x), 1)
    phases = ((cells * waves) & (total_x - 1)).astype(jnp.float32) * (2.0 * math.pi / total_x)
    scale = 1.0 / math.sqrt(total_x)
    cosine = jnp.cos(phases) * scale
    sine = jnp.sin(phases) * scale
    signed = jnp.where(waves < total_x // 2, waves, waves - total_x)
    rate = courant * signed.astype(jnp.float32) / (total_x // 2)
    quarters = (
        (cosine, -sine), (sine, cosine),
        (-rate * sine, -rate * cosine), (rate * cosine, -rate * sine),
    )
    for i, pair in enumerate(quarters):
        for j, values in enumerate(pair):
            where = (pl.ds(i * local_x, local_x), pl.ds(j * local_x, local_x))
            high, low = split(values)
            table[(0,) + where] = high
            table[(1,) + where] = low

    def absorb(i, group, fresh):
        for begin in range(0, len(group), 4):
            sums = [None] * 4
            for m in group[begin : begin + 4]:
                mine = gat[m, i] if m else v_ref[i]
                flux = mine * (gat[m, i % planes] if m else v_ref[i % planes])
                c, s = coef[0, m : m + 1, :], coef[1, m : m + 1, :]
                for k, term in enumerate((mine * c, mine * s, flux * c, flux * s)):
                    sums[k] = term if sums[k] is None else sums[k] + term
            for k in range(4):
                lanes = pl.ds(k * local_x, local_x)
                acc[i, :, lanes] = sums[k] if fresh and begin == 0 else acc[i, :, lanes] + sums[k]

    width = 2 * local_x
    per_item = width // chunk
    count = items * per_item

    def chain_copy(down, c):
        src, dst, send, recv = (d_out, d_in, d_send, d_recv) if down else (u_out, u_in, u_send, u_recv)
        to = jnp.minimum(z + 1, n_gy - 1) if down else jnp.maximum(z - 1, 0)
        return pltpu.make_async_remote_copy(
            src_ref=src.at[c], dst_ref=dst.at[c], send_sem=send.at[c], recv_sem=recv.at[c],
            device_id={"gy": to}, device_id_type=mesh_type,
        )

    def lanes_of(c):
        return c // per_item, pl.ds((c % per_item) * chunk, chunk)

    def finish(i):
        side = split(dot3(split(acc[i]), (table[0], table[1])))
        load = dot3(split(b_ref[...]), side)
        o_ref[i] = load
        for k in range(per_item):
            c = i * per_item + k
            d_out[c] = load[:, k * chunk : (k + 1) * chunk]
            u_out[c] = load[:, k * chunk : (k + 1) * chunk]

            if n_gy > 1:
                @pl.when(first)
                def _():
                    chain_copy(True, c).start()

                @pl.when(last)
                def _():
                    chain_copy(False, c).start()

    level_of = [[m for m in range(0, n_gx, 2) if m.bit_count() == h] for h in range(hops + 1)]
    events = sorted((2 * h + i, i, h) for h in range(1, hops + 1) for i in range(items))

    def complete(i):
        odd = [m | 1 for m in level_of[hops] if m | 1 < n_gx]
        for m in odd:
            for part in range(2):
                arrive(i, part, m)
        group = odd + ([0] if hops == 0 else [])
        absorb(i, group, hops == 0)
        finish(i)

    ready = []
    for at, (slot, i, h) in enumerate(events):
        forward(i, level_of[h])
        if h == 1 and i + 2 < items:
            forward(i + 2, [0])
        odd = [m | 1 for m in level_of[h - 1]]
        for m in odd:
            for part in range(2):
                arrive(i, part, m)
        absorb(i, ([0] if h == 1 else []) + odd + level_of[h], h == 1)
        if n_gy > 1 and at == min(1, len(events) - 1):
            pl.when(z == n_gy - 2)(g_step)
        for done in ready:
            complete(done)
        ready = [i] if h == hops else []
    if n_gy > 1 and not events:
        pl.when(z == n_gy - 2)(g_step)
    for done in ready if events else range(items):
        complete(done)

    def step_down(c):
        i, lanes = lanes_of(c)

        @pl.when(z > 0)
        def _():
            chain_copy(True, c).wait_recv()
            got = dot3(lower, split(d_in[c]))

            @pl.when(z < n_gy - 1)
            def _():
                d_out[c] = d_out[c] + got[:rows]
                chain_copy(True, c).start()

            o_ref[i, :, lanes] = o_ref[i, :, lanes] + got[rows:]

    def step_up(c):
        i, lanes = lanes_of(c)

        @pl.when(z < n_gy - 1)
        def _():
            chain_copy(False, c).wait_recv()
            got = dot3(upper, split(across[c] + u_in[c]))

            @pl.when(z > 0)
            def _():
                u_out[c] = u_out[c] + got
                chain_copy(False, c).start()

            o_ref[i, :, lanes] = o_ref[i, :, lanes] + got

    if n_gy > 1:
        if n_gy > 2:
            pl.when(z < n_gy - 2)(g_step)

        @pl.when(z < n_gy - 1)
        def _():
            below = split(g_in[...])
            for i in range(items):
                moved = dot3(below, split(o_ref[i]))
                for k in range(per_item):
                    across[i * per_item + k] = moved[:, k * chunk : (k + 1) * chunk]

        lag = min(3, count)
        upper = split(r_ref[...])

        @pl.when(first)
        def _():
            g_out[...] = jnp.zeros_like(g_out)

        lower = split(jnp.concatenate([l_ref[...], g_out[...]], 0))
        for early, late, here in (
            (step_down, step_up, z < n_gy // 2),
            (step_up, step_down, z >= n_gy // 2),
        ):
            @pl.when(here)
            def _():
                for s in range(count + lag):
                    if s < count:
                        early(s)
                    if s >= lag:
                        late(s - lag)

    for item in range(items):
        for part in range(2):
            for m in range(1, n_gx):
                bit = last_bit(part, m)
                copy(item, part, m ^ bit, bit).wait_send()
    if n_gy > 1:
        @pl.when(z > 0)
        def _():
            g_copy().wait_send()
            for c in range(count):
                chain_copy(False, c).wait_send()

        @pl.when(z < n_gy - 1)
        def _():
            for c in range(count):
                chain_copy(True, c).wait_send()


def shards(velocity, block_inverse, lower_map, upper_map):
    comps, planes, rows, local_x = velocity.shape
    n_gx, n_gy = lax.axis_size("gx"), lax.axis_size("gy")
    items = comps * planes
    chunk = local_x
    count = items * 2 * local_x // chunk
    f32, bf16 = jnp.float32, jnp.bfloat16
    vmem, dma = pltpu.VMEM, pltpu.SemaphoreType.DMA
    out = pl.pallas_call(
        functools.partial(kernel, n_gx, n_gy, chunk),
        out_shape=jax.ShapeDtypeStruct((items, rows, 2 * local_x), f32),
        in_specs=[pl.BlockSpec(memory_space=pl.ANY)] * 4,
        out_specs=pl.BlockSpec(memory_space=pltpu.VMEM),
        scratch_shapes=[
            vmem((items, rows, local_x), f32),
            vmem((rows, rows), f32),
            vmem((rows, rows), f32),
            vmem((rows, rows), f32),
            vmem((n_gx, items, rows, local_x), f32),
            vmem((2, max(n_gx, 8), local_x), f32),
            vmem((2, 4 * local_x, 2 * local_x), bf16),
            vmem((items, rows, 4 * local_x), f32),
            vmem((rows, rows), f32),
            vmem((rows, rows), f32),
            vmem((count, rows, chunk), f32),
            vmem((count, rows, chunk), f32),
            vmem((count, rows, chunk), f32),
            vmem((count, rows, chunk), f32),
            vmem((count, rows, chunk), f32),
            dma((items,)), dma((3,)),
            dma((items, 2, n_gx)), dma((items, 2, n_gx)), dma, dma,
            dma((count,)), dma((count,)), dma((count,)), dma((count,)),
        ],
        compiler_params=pltpu.CompilerParams(
            collective_id=0, has_side_effects=True, vmem_limit_bytes=67043328
        ),
        name="step",
    )(velocity.reshape(items, rows, local_x), block_inverse, lower_map, upper_map)
    return out.reshape(comps, planes, rows, 2 * local_x)


def solution(mesh):
    return jax.shard_map(
        shards,
        mesh=mesh,
        in_specs=(P(None, None, "gy", "gx"), P("gy", None), P("gy", None), P("gy", None)),
        out_specs=P(None, None, "gy", "gx"),
        check_vma=False,
    )
```

```python
import functools
import math

import jax
import jax.numpy as jnp
from jax import lax
from jax.experimental import pallas as pl
from jax.experimental.pallas import tpu as pltpu
from jax.sharding import PartitionSpec as P

courant = 0.8


def split(x):
    high = x.astype(jnp.bfloat16)
    return high, (x - high.astype(jnp.float32)).astype(jnp.bfloat16)


def dot3(a, b):
    dot = functools.partial(jnp.dot, preferred_element_type=jnp.float32)
    return dot(a[0], b[0]) + (dot(a[0], b[1]) + dot(a[1], b[0]))


def reversed_position(position, levels):
    result = position * 0
    for place in range(levels):
        result = result + ((position >> place) & 1) * (1 << (levels - 1 - place))
    return result


def kernel(
    n_gx, n_gy, chunk,
    v_hbm, b_hbm, l_hbm, r_hbm, o_ref,
    v_ref, b_ref, l_ref, r_ref, gat, coef, table, acc, g_in, g_out,
    d_in, d_out, u_in, u_out, across,
    own_sem, map_sem, gx_send, gx_recv, g_send, g_recv, d_send, d_recv, u_send, u_recv,
):
    items, rows, local_x = v_ref.shape
    planes = items // 3
    half = rows // 2
    levels = n_gx.bit_length() - 1
    hops = max(levels - 1, 0)
    total_x = local_x * n_gx
    me = lax.axis_index("gx")
    z = lax.axis_index("gy")
    lead = reversed_position(me, levels)
    first, last = z == 0, z == n_gy - 1
    mesh_type = pl.DeviceIdType.MESH

    own = [pltpu.make_async_copy(v_hbm.at[i], v_ref.at[i], own_sem.at[i]) for i in range(items)]
    maps = [
        pltpu.make_async_copy(src, dst, map_sem.at[i])
        for i, (src, dst) in enumerate(((l_hbm, l_ref), (r_hbm, r_ref), (b_hbm, b_ref)))
    ]
    for local in own + maps:
        local.start()

    barrier = pltpu.get_barrier_semaphore()
    for place in range(levels):
        pl.semaphore_signal(barrier, inc=1, device_id={"gx": me ^ (1 << place)}, device_id_type=mesh_type)

    @pl.when(z > 0)
    def _():
        pl.semaphore_signal(barrier, inc=1, device_id={"gy": z - 1}, device_id_type=mesh_type)

    @pl.when(z < n_gy - 1)
    def _():
        pl.semaphore_signal(barrier, inc=1, device_id={"gy": z + 1}, device_id_type=mesh_type)

    for local in own + maps:
        local.wait()
    peers = levels + jnp.where(z > 0, 1, 0) + jnp.where(z < n_gy - 1, 1, 0)
    pl.semaphore_wait(barrier, peers)

    outer = [1 << place for place in reversed(range(1, levels))]
    turn = len(outer) // 2
    orders = [outer + [1], outer[turn:] + outer[:turn] + [1]]

    def copy(item, part, mask, bit):
        span = pl.ds(part * half, half)
        return pltpu.make_async_remote_copy(
            src_ref=gat.at[mask, item, span, :] if mask else v_ref.at[item, span, :],
            dst_ref=gat.at[mask | bit, item, span, :],
            send_sem=gx_send.at[item, part, mask | bit],
            recv_sem=gx_recv.at[item, part, mask | bit],
            device_id={"gx": me ^ bit},
            device_id_type=mesh_type,
        )

    def last_bit(part, mask):
        return [bit for bit in orders[part] if mask & bit][-1]

    def arrive(item, part, mask):
        bit = last_bit(part, mask)
        copy(item, part, mask ^ bit, bit).wait_recv()

    def forward(item, masks):
        pieces = [(orders[part].index(last_bit(part, m)), part, m) for m in masks for part in range(2)]
        for place, part, mask in sorted(pieces):
            arrive(item, part, mask)
            for bit in orders[part][place + 1 :]:
                copy(item, part, mask, bit).start()

    def send_own(item, places):
        for place in places:
            for part in range(2):
                copy(item, part, 0, orders[part][place]).start()

    if n_gx > 1:
        for item in range(items):
            late = item >= 2 and hops > 0
            send_own(item, range(1) if late else range(levels))

    def g_copy():
        return pltpu.make_async_remote_copy(
            src_ref=g_out, dst_ref=g_in, send_sem=g_send, recv_sem=g_recv,
            device_id={"gy": jnp.maximum(z - 1, 0)}, device_id_type=mesh_type,
        )

    if n_gy > 1:
        @pl.when(last)
        def _():
            g_out[...] = l_ref[...]
            g_copy().start()

    def g_step():
        g_copy().wait_recv()

        @pl.when(z > 0)
        def _():
            low = l_ref[...]
            inner = dot3(split(g_in[...]), split(low))
            g_out[...] = low + dot3(split(r_ref[...]), split(inner))
            g_copy().start()

    masks = lax.broadcasted_iota(jnp.int32, coef.shape[1:], 0)
    turns = ((masks ^ me) * lead) & (n_gx - 1)
    angles = turns.astype(jnp.float32) * (2.0 * math.pi / n_gx)
    coef[0] = jnp.cos(angles)
    coef[1] = -jnp.sin(angles)
    cells = lax.broadcasted_iota(jnp.int32, (local_x, local_x), 0)
    waves = lead + n_gx * lax.broadcasted_iota(jnp.int32, (local_x, local_x), 1)
    phases = ((cells * waves) & (total_x - 1)).astype(jnp.float32) * (2.0 * math.pi / total_x)
    scale = 1.0 / math.sqrt(total_x)
    cosine = jnp.cos(phases) * scale
    sine = jnp.sin(phases) * scale
    signed = jnp.where(waves < total_x // 2, waves, waves - total_x)
    rate = courant * signed.astype(jnp.float32) / (total_x // 2)
    quarters = (
        (cosine, -sine), (sine, cosine),
        (-rate * sine, -rate * cosine), (rate * cosine, -rate * sine),
    )
    for i, pair in enumerate(quarters):
        for j, values in enumerate(pair):
            where = (pl.ds(i * local_x, local_x), pl.ds(j * local_x, local_x))
            high, low = split(values)
            table[(0,) + where] = high
            table[(1,) + where] = low

    def absorb(i, group, fresh):
        for begin in range(0, len(group), 4):
            sums = [None] * 4
            for m in group[begin : begin + 4]:
                mine = gat[m, i] if m else v_ref[i]
                flux = mine * (gat[m, i % planes] if m else v_ref[i % planes])
                c, s = coef[0, m : m + 1, :], coef[1, m : m + 1, :]
                for k, term in enumerate((mine * c, mine * s, flux * c, flux * s)):
                    sums[k] = term if sums[k] is None else sums[k] + term
            for k in range(4):
                lanes = pl.ds(k * local_x, local_x)
                acc[i, :, lanes] = sums[k] if fresh and begin == 0 else acc[i, :, lanes] + sums[k]

    width = 2 * local_x
    per_item = width // chunk
    count = items * per_item

    def chain_copy(down, c):
        src, dst, send, recv = (d_out, d_in, d_send, d_recv) if down else (u_out, u_in, u_send, u_recv)
        to = jnp.minimum(z + 1, n_gy - 1) if down else jnp.maximum(z - 1, 0)
        return pltpu.make_async_remote_copy(
            src_ref=src.at[c], dst_ref=dst.at[c], send_sem=send.at[c], recv_sem=recv.at[c],
            device_id={"gy": to}, device_id_type=mesh_type,
        )

    def lanes_of(c):
        return c // per_item, pl.ds((c % per_item) * chunk, chunk)

    def finish(i):
        side = split(dot3(split(acc[i]), (table[0], table[1])))
        load = dot3(split(b_ref[...]), side)
        o_ref[i] = load
        for k in range(per_item):
            c = i * per_item + k
            d_out[c] = load[:, k * chunk : (k + 1) * chunk]
            u_out[c] = load[:, k * chunk : (k + 1) * chunk]

            if n_gy > 1:
                @pl.when(first)
                def _():
                    chain_copy(True, c).start()

                @pl.when(last)
                def _():
                    chain_copy(False, c).start()

    level_of = [[m for m in range(0, n_gx, 2) if m.bit_count() == h] for h in range(hops + 1)]
    events = sorted((2 * h + i, i, h) for h in range(1, hops + 1) for i in range(items))

    def complete(i):
        odd = [m | 1 for m in level_of[hops] if m | 1 < n_gx]
        for m in odd:
            for part in range(2):
                arrive(i, part, m)
        group = odd + ([0] if hops == 0 else [])
        absorb(i, group, hops == 0)
        finish(i)

    ready = []
    for at, (slot, i, h) in enumerate(events):
        forward(i, level_of[h])
        if h == 1 and i + 2 < items:
            send_own(i + 2, range(1, levels))
        odd = [m | 1 for m in level_of[h - 1]]
        for m in odd:
            for part in range(2):
                arrive(i, part, m)
        absorb(i, ([0] if h == 1 else []) + odd + level_of[h], h == 1)
        if n_gy > 1 and at == min(1, len(events) - 1):
            pl.when(z == n_gy - 2)(g_step)
        for done in ready:
            complete(done)
        ready = [i] if h == hops else []
    if n_gy > 1 and not events:
        pl.when(z == n_gy - 2)(g_step)
    for done in ready if events else range(items):
        complete(done)

    def step_down(c):
        i, lanes = lanes_of(c)

        @pl.when(z > 0)
        def _():
            chain_copy(True, c).wait_recv()
            got = dot3(lower, split(d_in[c]))

            @pl.when(z < n_gy - 1)
            def _():
                d_out[c] = d_out[c] + got[:rows]
                chain_copy(True, c).start()

            o_ref[i, :, lanes] = o_ref[i, :, lanes] + got[rows:]

    def step_up(c):
        i, lanes = lanes_of(c)

        @pl.when(z < n_gy - 1)
        def _():
            chain_copy(False, c).wait_recv()
            got = dot3(upper, split(across[c] + u_in[c]))

            @pl.when(z > 0)
            def _():
                u_out[c] = u_out[c] + got
                chain_copy(False, c).start()

            o_ref[i, :, lanes] = o_ref[i, :, lanes] + got

    if n_gy > 1:
        if n_gy > 2:
            pl.when(z < n_gy - 2)(g_step)

        @pl.when(z < n_gy - 1)
        def _():
            below = split(g_in[...])
            for i in range(items):
                moved = dot3(below, split(o_ref[i]))
                for k in range(per_item):
                    across[i * per_item + k] = moved[:, k * chunk : (k + 1) * chunk]

        lag = min(3, count)
        upper = split(r_ref[...])

        @pl.when(first)
        def _():
            g_out[...] = jnp.zeros_like(g_out)

        lower = split(jnp.concatenate([l_ref[...], g_out[...]], 0))
        for early, late, here in (
            (step_down, step_up, z < n_gy // 2),
            (step_up, step_down, z >= n_gy // 2),
        ):
            @pl.when(here)
            def _():
                for s in range(count + lag):
                    if s < count:
                        early(s)
                    if s >= lag:
                        late(s - lag)

    for item in range(items):
        for part in range(2):
            for m in range(1, n_gx):
                bit = last_bit(part, m)
                copy(item, part, m ^ bit, bit).wait_send()
    if n_gy > 1:
        @pl.when(z > 0)
        def _():
            g_copy().wait_send()
            for c in range(count):
                chain_copy(False, c).wait_send()

        @pl.when(z < n_gy - 1)
        def _():
            for c in range(count):
                chain_copy(True, c).wait_send()


def shards(velocity, block_inverse, lower_map, upper_map):
    comps, planes, rows, local_x = velocity.shape
    n_gx, n_gy = lax.axis_size("gx"), lax.axis_size("gy")
    items = comps * planes
    chunk = local_x
    count = items * 2 * local_x // chunk
    f32, bf16 = jnp.float32, jnp.bfloat16
    vmem, dma = pltpu.VMEM, pltpu.SemaphoreType.DMA
    out = pl.pallas_call(
        functools.partial(kernel, n_gx, n_gy, chunk),
        out_shape=jax.ShapeDtypeStruct((items, rows, 2 * local_x), f32),
        in_specs=[pl.BlockSpec(memory_space=pl.ANY)] * 4,
        out_specs=pl.BlockSpec(memory_space=pltpu.VMEM),
        scratch_shapes=[
            vmem((items, rows, local_x), f32),
            vmem((rows, rows), f32),
            vmem((rows, rows), f32),
            vmem((rows, rows), f32),
            vmem((n_gx, items, rows, local_x), f32),
            vmem((2, max(n_gx, 8), local_x), f32),
            vmem((2, 4 * local_x, 2 * local_x), bf16),
            vmem((items, rows, 4 * local_x), f32),
            vmem((rows, rows), f32),
            vmem((rows, rows), f32),
            vmem((count, rows, chunk), f32),
            vmem((count, rows, chunk), f32),
            vmem((count, rows, chunk), f32),
            vmem((count, rows, chunk), f32),
            vmem((count, rows, chunk), f32),
            dma((items,)), dma((3,)),
            dma((items, 2, n_gx)), dma((items, 2, n_gx)), dma, dma,
            dma((count,)), dma((count,)), dma((count,)), dma((count,)),
        ],
        compiler_params=pltpu.CompilerParams(
            collective_id=0, has_side_effects=True, vmem_limit_bytes=67043328
        ),
        name="step",
    )(velocity.reshape(items, rows, local_x), block_inverse, lower_map, upper_map)
    return out.reshape(comps, planes, rows, 2 * local_x)


def solution(mesh):
    return jax.shard_map(
        shards,
        mesh=mesh,
        in_specs=(P(None, None, "gy", "gx"), P("gy", None), P("gy", None), P("gy", None)),
        out_specs=P(None, None, "gy", "gx"),
        check_vma=False,
    )
```

```python
import functools
import math

import jax
import jax.numpy as jnp
from jax import lax
from jax.experimental import pallas as pl
from jax.experimental.pallas import tpu as pltpu
from jax.sharding import PartitionSpec as P

courant = 0.8


def split(x):
    high = x.astype(jnp.bfloat16)
    return high, (x - high.astype(jnp.float32)).astype(jnp.bfloat16)


def dot3(a, b):
    dot = functools.partial(jnp.dot, preferred_element_type=jnp.float32)
    return dot(a[0], b[0]) + (dot(a[0], b[1]) + dot(a[1], b[0]))


def reversed_position(position, levels):
    result = position * 0
    for place in range(levels):
        result = result + ((position >> place) & 1) * (1 << (levels - 1 - place))
    return result


def kernel(
    n_gx, n_gy, chunk,
    v_hbm, b_hbm, l_hbm, r_hbm, o_ref,
    v_ref, b_ref, l_ref, r_ref, gat, coef, table, acc, g_in, g_out,
    d_in, d_out, u_in, u_out, across,
    own_sem, map_sem, gx_send, gx_recv, g_send, g_recv, d_send, d_recv, u_send, u_recv,
):
    items, rows, local_x = v_ref.shape
    planes = items // 3
    half = rows // 2
    levels = n_gx.bit_length() - 1
    hops = max(levels - 1, 0)
    total_x = local_x * n_gx
    me = lax.axis_index("gx")
    z = lax.axis_index("gy")
    lead = reversed_position(me, levels)
    first, last = z == 0, z == n_gy - 1
    mesh_type = pl.DeviceIdType.MESH

    own = [pltpu.make_async_copy(v_hbm.at[i], v_ref.at[i], own_sem.at[i]) for i in range(items)]
    maps = [
        pltpu.make_async_copy(src, dst, map_sem.at[i])
        for i, (src, dst) in enumerate(((l_hbm, l_ref), (r_hbm, r_ref), (b_hbm, b_ref)))
    ]
    for local in own + maps:
        local.start()

    barrier = pltpu.get_barrier_semaphore()
    for place in range(levels):
        pl.semaphore_signal(barrier, inc=1, device_id={"gx": me ^ (1 << place)}, device_id_type=mesh_type)

    @pl.when(z > 0)
    def _():
        pl.semaphore_signal(barrier, inc=1, device_id={"gy": z - 1}, device_id_type=mesh_type)

    @pl.when(z < n_gy - 1)
    def _():
        pl.semaphore_signal(barrier, inc=1, device_id={"gy": z + 1}, device_id_type=mesh_type)

    for local in own + maps:
        local.wait()
    peers = levels + jnp.where(z > 0, 1, 0) + jnp.where(z < n_gy - 1, 1, 0)
    pl.semaphore_wait(barrier, peers)

    outer = [1 << place for place in reversed(range(1, levels))]
    turn = len(outer) // 2
    orders = [outer + [1], outer[turn:] + outer[:turn] + [1]]

    def copy(item, part, mask, bit):
        span = pl.ds(part * half, half)
        return pltpu.make_async_remote_copy(
            src_ref=gat.at[mask, item, span, :] if mask else v_ref.at[item, span, :],
            dst_ref=gat.at[mask | bit, item, span, :],
            send_sem=gx_send.at[item, part, mask | bit],
            recv_sem=gx_recv.at[item, part, mask | bit],
            device_id={"gx": me ^ bit},
            device_id_type=mesh_type,
        )

    def last_bit(part, mask):
        return [bit for bit in orders[part] if mask & bit][-1]

    def arrive(item, part, mask):
        bit = last_bit(part, mask)
        copy(item, part, mask ^ bit, bit).wait_recv()

    def forward(item, masks):
        pieces = [(orders[part].index(last_bit(part, m)), part, m) for m in masks for part in range(2)]
        for place, part, mask in sorted(pieces):
            arrive(item, part, mask)
            for bit in orders[part][place + 1 :]:
                copy(item, part, mask, bit).start()

    def send_own(item, places):
        for place in places:
            for part in range(2):
                copy(item, part, 0, orders[part][place]).start()

    if n_gx > 1:
        for item in range(items):
            late = item >= 2 and hops > 0
            send_own(item, range(1) if late else range(levels))

    def g_copy():
        return pltpu.make_async_remote_copy(
            src_ref=g_out, dst_ref=g_in, send_sem=g_send, recv_sem=g_recv,
            device_id={"gy": jnp.maximum(z - 1, 0)}, device_id_type=mesh_type,
        )

    if n_gy > 1:
        @pl.when(last)
        def _():
            g_out[...] = l_ref[...]
            g_copy().start()

    def g_step():
        g_copy().wait_recv()

        @pl.when(z > 0)
        def _():
            low = l_ref[...]
            inner = dot3(split(g_in[...]), split(low))
            g_out[...] = low + dot3(split(r_ref[...]), split(inner))
            g_copy().start()

    masks = lax.broadcasted_iota(jnp.int32, coef.shape[1:], 0)
    turns = ((masks ^ me) * lead) & (n_gx - 1)
    angles = turns.astype(jnp.float32) * (2.0 * math.pi / n_gx)
    coef[0] = jnp.cos(angles)
    coef[1] = -jnp.sin(angles)
    cells = lax.broadcasted_iota(jnp.int32, (local_x, local_x), 0)
    waves = lead + n_gx * lax.broadcasted_iota(jnp.int32, (local_x, local_x), 1)
    phases = ((cells * waves) & (total_x - 1)).astype(jnp.float32) * (2.0 * math.pi / total_x)
    scale = 1.0 / math.sqrt(total_x)
    cosine = jnp.cos(phases) * scale
    sine = jnp.sin(phases) * scale
    signed = jnp.where(waves < total_x // 2, waves, waves - total_x)
    rate = courant * signed.astype(jnp.float32) / (total_x // 2)
    quarters = (
        (cosine, -sine), (sine, cosine),
        (-rate * sine, -rate * cosine), (rate * cosine, -rate * sine),
    )
    for i, pair in enumerate(quarters):
        for j, values in enumerate(pair):
            where = (pl.ds(i * local_x, local_x), pl.ds(j * local_x, local_x))
            high, low = split(values)
            table[(0,) + where] = high
            table[(1,) + where] = low

    def absorb(i, group, fresh):
        for begin in range(0, len(group), 4):
            sums = [None] * 4
            for m in group[begin : begin + 4]:
                mine = gat[m, i] if m else v_ref[i]
                flux = mine * (gat[m, i % planes] if m else v_ref[i % planes])
                c, s = coef[0, m : m + 1, :], coef[1, m : m + 1, :]
                for k, term in enumerate((mine * c, mine * s, flux * c, flux * s)):
                    sums[k] = term if sums[k] is None else sums[k] + term
            for k in range(4):
                lanes = pl.ds(k * local_x, local_x)
                acc[i, :, lanes] = sums[k] if fresh and begin == 0 else acc[i, :, lanes] + sums[k]

    width = 2 * local_x
    per_item = width // chunk
    count = items * per_item

    def chain_copy(down, c):
        src, dst, send, recv = (d_out, d_in, d_send, d_recv) if down else (u_out, u_in, u_send, u_recv)
        to = jnp.minimum(z + 1, n_gy - 1) if down else jnp.maximum(z - 1, 0)
        return pltpu.make_async_remote_copy(
            src_ref=src.at[c], dst_ref=dst.at[c], send_sem=send.at[c], recv_sem=recv.at[c],
            device_id={"gy": to}, device_id_type=mesh_type,
        )

    def lanes_of(c):
        return c // per_item, pl.ds((c % per_item) * chunk, chunk)

    def finish(i):
        side = split(dot3(split(acc[i]), (table[0], table[1])))
        load = dot3(split(b_ref[...]), side)
        o_ref[i] = load
        for k in range(per_item):
            c = i * per_item + k
            d_out[c] = load[:, k * chunk : (k + 1) * chunk]
            u_out[c] = load[:, k * chunk : (k + 1) * chunk]

            if n_gy > 1:
                @pl.when(first)
                def _():
                    chain_copy(True, c).start()

                @pl.when(last)
                def _():
                    chain_copy(False, c).start()

    level_of = [[m for m in range(0, n_gx, 2) if m.bit_count() == h] for h in range(hops + 1)]
    events = sorted((2 * h + i, i, h) for h in range(1, hops + 1) for i in range(items))

    def complete(i):
        odd = [m | 1 for m in level_of[hops] if m | 1 < n_gx]
        for m in odd:
            for part in range(2):
                arrive(i, part, m)
        group = odd + ([0] if hops == 0 else [])
        absorb(i, group, hops == 0)
        finish(i)

    ready = []
    for at, (slot, i, h) in enumerate(events):
        forward(i, level_of[h])
        if h == 1 and i + 2 < items:
            send_own(i + 2, range(1, levels))
        odd = [m | 1 for m in level_of[h - 1]]
        for m in odd:
            for part in range(2):
                arrive(i, part, m)
        absorb(i, ([0] if h == 1 else []) + odd + level_of[h], h == 1)
        if n_gy > 1 and at == min(1, len(events) - 1):
            pl.when(z == n_gy - 2)(g_step)
        for done in ready:
            complete(done)
        ready = [i] if h == hops else []
    if n_gy > 1 and not events:
        pl.when(z == n_gy - 2)(g_step)
    for done in ready if events else range(items):
        complete(done)

    def step_down(c):
        i, lanes = lanes_of(c)

        @pl.when(z > 0)
        def _():
            chain_copy(True, c).wait_recv()
            got = dot3(lower, split(d_in[c]))

            @pl.when(z < n_gy - 1)
            def _():
                d_out[c] = d_out[c] + got[:rows]
                chain_copy(True, c).start()

            o_ref[i, :, lanes] = o_ref[i, :, lanes] + got[rows:]

    def step_up(c):
        i, lanes = lanes_of(c)

        @pl.when(z < n_gy - 1)
        def _():
            chain_copy(False, c).wait_recv()
            got = dot3(upper, split(across[c] + u_in[c]))

            @pl.when(z > 0)
            def _():
                u_out[c] = u_out[c] + got
                chain_copy(False, c).start()

            o_ref[i, :, lanes] = o_ref[i, :, lanes] + got

    if n_gy > 1:
        if n_gy > 2:
            pl.when(z < n_gy - 2)(g_step)

        @pl.when(z < n_gy - 1)
        def _():
            below = split(g_in[...])
            for i in range(items):
                moved = dot3(below, split(o_ref[i]))
                for k in range(per_item):
                    across[i * per_item + k] = moved[:, k * chunk : (k + 1) * chunk]

        lag = min(3, count)
        upper = split(r_ref[...])

        @pl.when(first)
        def _():
            g_out[...] = jnp.zeros_like(g_out)

        lower = split(jnp.concatenate([l_ref[...], g_out[...]], 0))
        for early, late, here in (
            (step_down, step_up, z < n_gy // 2),
            (step_up, step_down, z >= n_gy // 2),
        ):
            @pl.when(here)
            def _():
                for s in range(count + lag):
                    if s < count:
                        early(s)
                    if s >= lag:
                        late(s - lag)

    for item in range(items):
        for part in range(2):
            for m in range(1, n_gx):
                bit = last_bit(part, m)
                copy(item, part, m ^ bit, bit).wait_send()
    if n_gy > 1:
        @pl.when(z > 0)
        def _():
            g_copy().wait_send()
            for c in range(count):
                chain_copy(False, c).wait_send()

        @pl.when(z < n_gy - 1)
        def _():
            for c in range(count):
                chain_copy(True, c).wait_send()


def shards(velocity, block_inverse, lower_map, upper_map):
    comps, planes, rows, local_x = velocity.shape
    n_gx, n_gy = lax.axis_size("gx"), lax.axis_size("gy")
    items = comps * planes
    chunk = local_x
    count = items * 2 * local_x // chunk
    f32, bf16 = jnp.float32, jnp.bfloat16
    vmem, dma = pltpu.VMEM, pltpu.SemaphoreType.DMA
    out = pl.pallas_call(
        functools.partial(kernel, n_gx, n_gy, chunk),
        out_shape=vmem((items, rows, 2 * local_x), f32),
        in_specs=[pl.BlockSpec(memory_space=pl.ANY)] * 4,
        out_specs=pl.BlockSpec(memory_space=pltpu.VMEM),
        scratch_shapes=[
            vmem((items, rows, local_x), f32),
            vmem((rows, rows), f32),
            vmem((rows, rows), f32),
            vmem((rows, rows), f32),
            vmem((n_gx, items, rows, local_x), f32),
            vmem((2, max(n_gx, 8), local_x), f32),
            vmem((2, 4 * local_x, 2 * local_x), bf16),
            vmem((items, rows, 4 * local_x), f32),
            vmem((rows, rows), f32),
            vmem((rows, rows), f32),
            vmem((count, rows, chunk), f32),
            vmem((count, rows, chunk), f32),
            vmem((count, rows, chunk), f32),
            vmem((count, rows, chunk), f32),
            vmem((count, rows, chunk), f32),
            dma((items,)), dma((3,)),
            dma((items, 2, n_gx)), dma((items, 2, n_gx)), dma, dma,
            dma((count,)), dma((count,)), dma((count,)), dma((count,)),
        ],
        compiler_params=pltpu.CompilerParams(
            collective_id=0, has_side_effects=True, vmem_limit_bytes=67108864 - 1000 * 1024
        ),
        name="step",
    )(velocity.reshape(items, rows, local_x), block_inverse, lower_map, upper_map)
    return out.reshape(comps, planes, rows, 2 * local_x)


def solution(mesh):
    return jax.shard_map(
        shards,
        mesh=mesh,
        in_specs=(P(None, None, "gy", "gx"), P("gy", None), P("gy", None), P("gy", None)),
        out_specs=P(None, None, "gy", "gx"),
        check_vma=False,
    )
```
